512 devices in a mesh: pair: 64 (over x, z), virt: 8 (over y, core).
Axes of the slice: x: 4, y: 4, z: 16, core: 2. Of those that a mesh axis runs over, the one named last changes fastest.
Arguments:
- t2_amplitudes: float32 [256, 8192], P('pair', 'virt'), may hold values from -6 to 6
- integral_tiles: float32 [64, 8, 32, 128, 128], P('pair', 'virt'), may hold values from -0.0625 to 0.0625
- out_tiles: int32 [64, 8, 32], P('pair', 'virt'), may hold values from 0 to 63, as said below
- in_tiles: int32 [64, 8, 32], P('pair', 'virt'), may hold values from 0 to 63
- tile_counts: int32 [64, 8], P('pair', 'virt'), may hold values from 1 to 32, as said below
Outputs:
- ladder: float32 [256, 8192], P('pair', 'virt')
The draws below stay inside these ranges and needn't reach their ends.
Inputs may be any that keep to these rules, and one draw needn't show every extreme that they name: `out_tiles`: slots of the devices at virt index v name output tiles v * 8 to (v + 1) * 8 - 1 only. `tile_counts`: in every draw some device has all 32 slots live.
All inputs are finite; a program needn't handle non-finite values.
Results may differ from the reference program's by a relative error of at most 0.0003.
Values sent between devices are 32-bit elements; how exact they have to be, the bound alone decides.
A program may use at most 64 MiB of HBM per device.

```python
import jax
import jax.numpy as jnp
from jax import lax

W = 128
KV = 8
LIST = 32
KG = 64
P_SIZE = 256
N_PAIR = 64
N_VIRT = 8


def draw_tile_counts(key, part):
    first_key, second_key = jax.random.split(jax.random.fold_in(key, 11))
    base_counts = jax.random.randint(first_key, (N_PAIR, N_VIRT), 1, LIST // 2 + 1)
    hot_rows = jax.random.randint(second_key, (N_VIRT,), 0, N_PAIR)
    hot_mask = jnp.arange(N_PAIR)[:, None] == hot_rows[None, :]
    return jnp.where(hot_mask, LIST, base_counts).astype(jnp.int32)


def draw_out_tiles(key, part):
    virt_index = jnp.arange(N_VIRT, dtype=jnp.int32)[None, :, None]
    picks = jax.random.randint(jax.random.fold_in(key, 23), (N_PAIR, N_VIRT, LIST), 0, KV)
    return (virt_index * KV + picks).astype(jnp.int32)


def with_ends(drawn, rng, smallest, largest):
    longest = drawn.shape.index(max(drawn.shape))
    spots = []
    for shift in (0, 1):
        where = [jax.random.randint(jax.random.fold_in(rng, axis), (), 0, length) for axis, length in enumerate(drawn.shape)]
        where[longest] = (where[longest] + shift) % drawn.shape[longest]
        spots.append(tuple(where))
    return drawn.at[spots[0]].set(smallest).at[spots[1]].set(largest)


def block_scale(stream_key, extent, pieces, smallest, high):
    def one(axis_at, blocks):
        steps = jax.random.uniform(jax.random.fold_in(jax.random.fold_in(stream_key, 6), axis_at), (blocks,), jnp.float32, smallest / len(pieces), high / len(pieces))
        return jnp.repeat(jnp.exp(steps), extent[axis_at] // blocks).reshape((-1,) + (1,) * (len(extent) - axis_at - 1))

    level = one(*pieces[0])
    for cut in pieces[1:]:
        level = level * one(*cut)
    return level


def gaussian(rng, shape, width, limit, shards=(), held_as=jnp.bfloat16):
    values = width * jax.random.normal(rng, shape, jnp.float32)
    if shards:
        values = values * block_scale(rng, shape, shards, -0.22, 0.18)
    return jnp.clip(values, -limit, limit).astype(held_as)


def setup_inputs(seed: int = 0) -> dict:
    key_of = jax.random.split(jax.random.key(seed), 6)
    return {
        "t2_amplitudes": gaussian(key_of[0], (P_SIZE, KG * W), 1.0, 6.0, ((0, 64), (1, 8)), jnp.float32),
        "integral_tiles": gaussian(key_of[1], (N_PAIR, N_VIRT, LIST, W, W), (W * N_PAIR * LIST // (4 * KV)) ** -0.5, 0.0625, ((0, 64), (1, 8)), jnp.float32),
        "out_tiles": draw_out_tiles(jax.random.fold_in(key_of[5], 71), 0),
        "in_tiles": with_ends(jax.random.randint(key_of[3], (N_PAIR, N_VIRT, LIST), 0, KG), jax.random.fold_in(key_of[3], 1), 0, KG - 1).astype(jnp.int32),
        "tile_counts": draw_tile_counts(jax.random.fold_in(key_of[5], 71), 0),
    }


def reference(t2_amplitudes, integral_tiles, out_tiles, in_tiles, tile_counts):
    row_count = t2_amplitudes.shape[0]
    blocks = t2_amplitudes.reshape(row_count, KG, W)
    flat_tiles = integral_tiles.reshape(N_PAIR * N_VIRT, LIST, W, W)
    flat_outs = out_tiles.reshape(N_PAIR * N_VIRT, LIST)
    flat_ins = in_tiles.reshape(N_PAIR * N_VIRT, LIST)
    flat_counts = tile_counts.reshape(N_PAIR * N_VIRT)
    virt_ids = jnp.tile(jnp.arange(N_VIRT, dtype=jnp.int32), N_PAIR)

    def owner(totals, packed):
        tiles, outs, ins, count, virt_index = packed
        columns = jnp.take(blocks, ins, axis=1)
        product = jnp.einsum("psc,sca->psa", columns, tiles, precision=lax.Precision.HIGHEST)
        is_live = jnp.arange(LIST, dtype=jnp.int32) < count
        local_tiles = outs - virt_index * KV
        selector = ((local_tiles[:, None] == jnp.arange(KV, dtype=jnp.int32)[None, :]) & is_live[:, None]).astype(jnp.float32)
        part_sum = jnp.einsum("psa,sk->pka", product, selector, precision=lax.Precision.HIGHEST)
        offset = (virt_index * KV).astype(jnp.int32)
        current = lax.dynamic_slice_in_dim(totals, offset, KV, 1)
        totals = lax.dynamic_update_slice_in_dim(totals, current + part_sum, offset, 1)
        return totals, None

    start_totals = jnp.zeros((row_count, KG, W), jnp.float32)
    totals, unused = lax.scan(owner, start_totals, (flat_tiles, flat_outs, flat_ins, flat_counts, virt_ids))
    return totals.reshape(row_count, KG * W)
```

```python
import jax
import jax.numpy as jnp
from jax import lax
from jax.experimental import pallas as pl
from jax.experimental.pallas import tpu as pltpu
from jax.sharding import PartitionSpec as P

W = 128
LIST = 32
NX = 4
NY = 4
NZ = 16
SLOTS = 2 * LIST
MESH = pl.DeviceIdType.MESH
F32 = jnp.float32
I32 = jnp.int32
BF = jnp.bfloat16


def schedule(meta_out, meta_in, counts, sched):
    lane = lax.broadcasted_iota(I32, (W, W), 1)
    sub = lax.broadcasted_iota(I32, (W, W), 0)
    eye = lane == sub
    lane_row = lax.broadcasted_iota(I32, (1, W), 1)
    core = lane_row // LIST
    key_row = jnp.where(lane_row - core * LIST < counts, meta_out, 16)
    key_row = jnp.where(lane_row < SLOTS, key_row, 17)
    keys = jnp.broadcast_to(key_row, (W, W))
    key_col = jnp.sum(jnp.where(eye, keys, 0), axis=1, keepdims=True)
    in_col = jnp.sum(jnp.where(eye, jnp.broadcast_to(meta_in, (W, W)), 0), axis=1, keepdims=True)
    below = jnp.sum((keys < key_col).astype(I32), axis=1, keepdims=True)
    ties = jnp.sum(((keys == key_col) & (lane < sub)).astype(I32), axis=1, keepdims=True)
    rank_col = below + ties
    hot = (rank_col == lane).astype(I32)
    slot_row = jnp.sum(hot * sub, axis=0, keepdims=True)
    in_row = jnp.sum(hot * in_col, axis=0, keepdims=True)
    keep_row = jnp.sum(hot * (ties > 0).astype(I32), axis=0, keepdims=True)
    upto = jnp.sum((key_col <= lane).astype(I32), axis=0, keepdims=True)
    here = jnp.sum((key_col == lane).astype(I32), axis=0, keepdims=True)
    last_row = jnp.where(here > 0, upto - 1, SLOTS)
    sched[0:1, :] = slot_row
    sched[1:2, :] = in_row
    sched[2:3, :] = keep_row
    sched[3:4, :] = last_row


def kernel(
    t2_ref, tiles_ref, outs_ref, ins_ref, count_ref, out_ref,
    rows, stage, slab, tiles, meta, sched, plan, sums, acc,
    rx1, rx2, zsrc, zbuf, zrecv, fin,
    swap_send, swap_recv, tile_send, tile_recv, local_sem, plan_sem,
    zg_send, zg_recv, ex_send, ex_recv, rx_send, rx_recv, zr_send, zr_recv,
):
    pair = lax.axis_index("pair")
    virt = lax.axis_index("virt")
    x, z = pair // NZ, pair % NZ
    y, c = virt // 2, virt % 2
    zr = {"pair": x * NZ + (z + 1) % NZ, "virt": virt}
    zl = {"pair": x * NZ + (z + NZ - 1) % NZ, "virt": virt}
    xr = {"pair": (x + 1) % NX * NZ + z, "virt": virt}
    xl = {"pair": (x + NX - 1) % NX * NZ + z, "virt": virt}
    yr = {"pair": pair, "virt": (y + 1) % NY * 2 + c}
    yl = {"pair": pair, "virt": (y + NY - 1) % NY * 2 + c}
    mate = {"pair": pair, "virt": y * 2 + 1 - c}

    def copy(src, dst, send, recv, device):
        return pltpu.make_async_remote_copy(
            src_ref=src, dst_ref=dst, send_sem=send, recv_sem=recv, device_id=device, device_id_type=MESH
        )

    barrier = pltpu.get_barrier_semaphore()
    for peer in (zr, zl, xr, xl, yr, yl, mate):
        pl.semaphore_signal(barrier, inc=1, device_id=peer, device_id_type=MESH)

    for row in range(4):
        for j in range(8):
            at = (row % 2) * 8 + j
            rows[row // 2, at : at + 1, :] = t2_ref[row : row + 1, j * W : (j + 1) * W]
    base = pl.multiple_of(z * 32, 32)
    mine = pl.multiple_of(c * 8, 8)
    for r in range(2):
        stage[pl.ds(base + r * 16 + mine, 8), :] = rows[c, r * 8 : r * 8 + 8, :]
    pad = jnp.zeros((1, W - LIST), I32)
    first = virt // 2 * 16
    meta[c, 0:1, :] = jnp.concatenate([outs_ref[0] - first, pad], axis=1)
    meta[c, 1:2, :] = jnp.concatenate([ins_ref[0], pad], axis=1)
    meta[c, 2:3, :] = jnp.broadcast_to(count_ref[0:1, 0:1], (1, W))
    pl.semaphore_wait(barrier, 7)

    swaps = []
    for r in range(2):
        part = stage.at[pl.ds(base + r * 16 + mine, 8), :]
        swaps.append(copy(rows.at[1 - c, pl.ds(r * 8, 8), :], part, swap_send.at[r], swap_recv.at[r], mate))
    swaps.append(copy(meta.at[c], meta.at[c], swap_send.at[2], swap_recv.at[2], mate))
    for one in swaps:
        one.start()
    theirs = pl.multiple_of((1 - c) * 8, 8)
    for r in range(2):
        part = stage.at[pl.ds(base + r * 16 + theirs, 8), :]
        copy(rows.at[1 - c, pl.ds(r * 8, 8), :], part, swap_send.at[r], swap_recv.at[r], mate).wait_recv()

    def chunk(q):
        return stage.at[pl.ds(pl.multiple_of(q % NZ * 32, 32), 32), :]

    def z_right(step, origin):
        return copy(chunk(origin), chunk(origin), zg_send.at[0, step], zg_recv.at[0, step], zr)

    def z_left(step, origin):
        return copy(chunk(origin), chunk(origin), zg_send.at[1, step], zg_recv.at[1, step], zl)

    for step in range(8):
        z_right(step, z + NZ - step).start()
        if step < 7:
            z_left(step, z + step).start()
        if step == 0:
            local = pltpu.make_async_copy(tiles_ref, tiles.at[pl.ds(c * LIST, LIST)], local_sem)
            local.start()
            across = copy(tiles_ref, tiles.at[pl.ds(c * LIST, LIST)], tile_send, tile_recv, mate)
            across.start()
        z_right(step, z + 2 * NZ - 1 - step).wait_recv()
        if step < 7:
            z_left(step, z + 1 + step).wait_recv()

    here = pl.multiple_of(x * 32, 32)

    def relayout(t, _):
        for r in range(2):
            slab[y, t, pl.ds(here + r * 16, 16), :] = stage[pl.ds(r * 16 + t, 16, stride=32), :]
        return 0

    lax.fori_loop(0, 16, relayout, 0)

    def x_rows(q):
        return pl.ds(pl.multiple_of(q * 32, 32), 32)

    def sel_0(h, q):
        return slab.at[y, pl.ds(4 * h, 4), x_rows(q), :]

    def sel_1(h, q):
        return slab.at[q, pl.ds(8 + 4 * h, 4), x_rows(x), :]

    def sel_2(h, q):
        return slab.at[q, pl.ds(4 * h, 4), :, :]

    def sel_3(h, q):
        return slab.at[:, pl.ds(8 + 4 * h, 4), x_rows(q), :]

    sels = (sel_0, sel_1, sel_2, sel_3)
    spots = (x, y, y, x)
    rights = (xr, yr, yr, xr)
    lefts = (xl, yl, yl, xl)

    def ex(n, k, h, q, device):
        ref = sels[n](h, q)
        return copy(ref, ref, ex_send.at[n, k], ex_recv.at[n, k], device)

    def sent(n, k):
        q = spots[n]
        q = (q, q, q, q, (q + 3) % 4, (q + 1) % 4)[k]
        return ex(n, k, (0, 1, 1, 0, 0, 1)[k], q, (rights, lefts)[k % 2][n])

    def got(n, k):
        q = spots[n]
        before, after, far = (q + 3) % 4, (q + 1) % 4, (q + 2) % 4
        q = (before, after, before, after, far, far)[k]
        return ex(n, k, (0, 1, 1, 0, 0, 1)[k], q, (rights, lefts)[k % 2][n])

    def run(pairs, between):
        for k in range(4):
            for n in pairs:
                sent(n, k).start()
        between()
        for k in range(2):
            for n in pairs:
                got(n, k).wait_recv()
                sent(n, 4 + k).start()
        for k in range(2, 6):
            for n in pairs:
                got(n, k).wait_recv()

    def prepare():
        copy(meta.at[c], meta.at[1 - c], swap_send.at[2], swap_recv.at[2], mate).wait_recv()
        low = lax.broadcasted_iota(I32, (1, W), 1) < LIST
        both = [
            jnp.where(low, meta[0, k : k + 1, :], pltpu.roll(meta[1, k : k + 1, :], LIST, 1)) for k in range(3)
        ]
        schedule(both[0], both[1], both[2], sched)
        turn = pltpu.make_async_copy(sched, plan, plan_sem)
        turn.start()
        turn.wait()

    run((0, 1), lambda: None)
    run((2, 3), prepare)
    local.wait()
    copy(tiles_ref, tiles.at[pl.ds((1 - c) * LIST, LIST)], tile_send, tile_recv, mate).wait_recv()

    sums[SLOTS] = jnp.zeros((W, W), F32)

    def slot(k, total):
        a = slab[plan[1, k] // 16, plan[1, k] % 16]
        b = tiles[plan[0, k]]
        keep = plan[2, k].astype(F32)
        a_high = a.astype(BF)
        a_low = (a - a_high.astype(F32)).astype(BF)
        b_high = b.astype(BF)
        b_low = (b - b_high.astype(F32)).astype(BF)
        left = jnp.concatenate([a_high, a_low], axis=1)
        right = jnp.concatenate([b_high, b_low], axis=1)
        right = jnp.concatenate([right, right], axis=0)
        product = jnp.dot(left, right, preferred_element_type=F32)
        total = total * keep + (product[:, :W] + product[:, W:])
        sums[k] = total
        return total

    lax.fori_loop(0, SLOTS, slot, jnp.zeros((W, W), F32))

    def pick(t, _):
        acc[t] = sums[plan[3, t]]
        return 0

    lax.fori_loop(0, 16, pick, 0)

    right_x, left_x, far_x = (x + 1) % NX, (x + 3) % NX, (x + 2) % NX

    def lot(lo, size, q):
        return acc.at[pl.ds(lo, size), x_rows(q), :]

    sums_x = [
        copy(lot(0, 8, far_x), rx1.at[0], rx_send.at[0], rx_recv.at[0], xr),
        copy(lot(8, 8, far_x), rx1.at[1], rx_send.at[1], rx_recv.at[1], xl),
        copy(lot(8, 8, right_x), rx2.at[0, pl.ds(8, 8)], rx_send.at[2], rx_recv.at[2], xr),
        copy(lot(0, 8, left_x), rx2.at[1, pl.ds(0, 8)], rx_send.at[3], rx_recv.at[3], xl),
        copy(lot(0, 8, right_x), rx2.at[0, pl.ds(0, 8)], rx_send.at[4], rx_recv.at[4], xr),
        copy(lot(8, 8, left_x), rx2.at[1, pl.ds(8, 8)], rx_send.at[5], rx_recv.at[5], xl),
    ]
    for one in sums_x[:4]:
        one.start()
    sums_x[0].wait_recv()

    def add_right(t, _):
        acc[t, x_rows(right_x), :] += rx1[0, t]
        return 0

    lax.fori_loop(0, 8, add_right, 0)
    sums_x[4].start()
    sums_x[1].wait_recv()

    def add_left(t, _):
        acc[8 + t, x_rows(left_x), :] += rx1[1, t]
        return 0

    lax.fori_loop(0, 8, add_left, 0)
    sums_x[5].start()
    for one in sums_x[2:]:
        one.wait_recv()

    def add_here(t, _):
        zsrc[pl.ds(pl.multiple_of(t * 32, 32), 32), :] = acc[t, x_rows(x), :] + rx2[0, t] + rx2[1, t]
        return 0

    lax.fori_loop(0, 16, add_here, 0)

    def split(q, _):
        for r in range(2):
            zbuf[q, r * 16 : r * 16 + 16, :] = zsrc[pl.ds(r * 16 + q, 16, stride=32), :]
        return 0

    lax.fori_loop(0, NZ, split, 0)

    def sum_right(step):
        q = (z + NZ + 8 - step) % NZ
        return copy(zbuf.at[q], zrecv.at[0, step], zr_send.at[0, step], zr_recv.at[0, step], zr)

    def sum_left(step):
        q = (z + NZ - 7 + step) % NZ
        return copy(zbuf.at[q], zrecv.at[1, step], zr_send.at[1, step], zr_recv.at[1, step], zl)

    for step in range(8):
        if step > 0:
            sum_right(step - 1).wait_recv()
            q = (z + NZ + 8 - step) % NZ
            zbuf[q] += zrecv[0, step - 1]
        sum_right(step).start()
        if step < 7:
            if step > 0:
                sum_left(step - 1).wait_recv()
                q = (z + NZ - 7 + step) % NZ
                zbuf[q] += zrecv[1, step - 1]
            sum_left(step).start()
    sum_right(7).wait_recv()
    sum_left(6).wait_recv()
    zbuf[z] += zrecv[0, 7] + zrecv[1, 6]

    for r in range(2):
        fin[c, r * 8 : r * 8 + 8, :] = zbuf[z, pl.ds(r * 16 + mine, 8), :]
    last = [
        copy(zbuf.at[z, pl.ds(r * 16 + theirs, 8), :], fin.at[c, pl.ds(r * 8, 8), :], swap_send.at[3 + r], swap_recv.at[3 + r], mate)
        for r in range(2)
    ]
    for one in last:
        one.start()
    for r in range(2):
        copy(zbuf.at[z, pl.ds(r * 16 + theirs, 8), :], fin.at[1 - c, pl.ds(r * 8, 8), :], swap_send.at[3 + r], swap_recv.at[3 + r], mate).wait_recv()
    for row in range(4):
        for j in range(8):
            at = (row % 2) * 8 + j
            out_ref[row : row + 1, j * W : (j + 1) * W] = fin[row // 2, at : at + 1, :]

    for one in swaps + last + sums_x:
        one.wait_send()
    across.wait_send()
    for step in range(8):
        z_right(step, z + NZ - step).wait_send()
        sum_right(step).wait_send()
        if step < 7:
            z_left(step, z + step).wait_send()
            sum_left(step).wait_send()
    for n in range(4):
        for k in range(6):
            sent(n, k).wait_send()


def shards(t2_amplitudes, integral_tiles, out_tiles, in_tiles, tile_counts):
    vmem = pl.BlockSpec(memory_space=pltpu.VMEM)
    dma = pltpu.SemaphoreType.DMA
    return pl.pallas_call(
        kernel,
        out_shape=jax.ShapeDtypeStruct(t2_amplitudes.shape, F32),
        in_specs=[vmem, pl.BlockSpec(memory_space=pltpu.HBM), vmem, vmem, vmem],
        out_specs=vmem,
        scratch_shapes=[
            pltpu.VMEM((2, 16, W), F32),
            pltpu.VMEM((NZ * 32, W), F32),
            pltpu.VMEM((NY, 16, W, W), F32),
            pltpu.VMEM((SLOTS, W, W), F32),
            pltpu.VMEM((2, 8, W), I32),
            pltpu.VMEM((8, W), I32),
            pltpu.SMEM((8, W), I32),
            pltpu.VMEM((SLOTS + 1, W, W), F32),
            pltpu.VMEM((16, W, W), F32),
            pltpu.VMEM((2, 8, 32, W), F32),
            pltpu.VMEM((2, 16, 32, W), F32),
            pltpu.VMEM((16 * 32, W), F32),
            pltpu.VMEM((NZ, 32, W), F32),
            pltpu.VMEM((2, 8, 32, W), F32),
            pltpu.VMEM((2, 16, W), F32),
            dma((5,)), dma((5,)), dma, dma, dma, dma,
            dma((2, 8)), dma((2, 8)), dma((4, 6)), dma((4, 6)), dma((6,)), dma((6,)), dma((2, 8)), dma((2, 8)),
        ],
        compiler_params=pltpu.CompilerParams(
            collective_id=0, has_side_effects=True, vmem_limit_bytes=48 * 1024 * 1024
        ),
    )(t2_amplitudes, integral_tiles.reshape(LIST, W, W), out_tiles, in_tiles, tile_counts)


def solution(mesh):
    return jax.shard_map(
        shards,
        mesh=mesh,
        in_specs=(
            P("pair", "virt"),
            P("pair", "virt", None, None, None),
            P("pair", "virt", None),
            P("pair", "virt", None),
            P("pair", "virt"),
        ),
        out_specs=P("pair", "virt"),
        check_vma=False,
    )
```

```python
import jax
import jax.numpy as jnp
from jax import lax
from jax.experimental import pallas as pl
from jax.experimental.pallas import tpu as pltpu
from jax.sharding import PartitionSpec as P

W = 128
LIST = 32
NX = 4
NY = 4
NZ = 16
SLOTS = 2 * LIST
MESH = pl.DeviceIdType.MESH
F32 = jnp.float32
I32 = jnp.int32
BF = jnp.bfloat16
DELTAS = (0, 1, -1, 2, -2, 3, -3, 4, -4, 5, -5, 6, -6, 7, -7, 8)
SLOT_OF = {d: i for i, d in enumerate(DELTAS)}
SLOT_OF[-8] = SLOT_OF[8]
GROUPS = ((0, 9), (9, 16))


def schedule(key_row, in_row, sched):
    lane = lax.broadcasted_iota(I32, (W, W), 1)
    sub = lax.broadcasted_iota(I32, (W, W), 0)
    eye = lane == sub
    keys = jnp.broadcast_to(key_row, (W, W))
    key_col = jnp.sum(jnp.where(eye, keys, 0), axis=1, keepdims=True)
    in_col = jnp.sum(jnp.where(eye, jnp.broadcast_to(in_row, (W, W)), 0), axis=1, keepdims=True)
    below = jnp.sum((keys < key_col).astype(I32), axis=1, keepdims=True)
    ties = jnp.sum(((keys == key_col) & (lane < sub)).astype(I32), axis=1, keepdims=True)
    hot = ((below + ties) == lane).astype(I32)
    tile = lane + lane // 8
    upto = jnp.sum((key_col <= tile).astype(I32), axis=0, keepdims=True)
    here = jnp.sum((key_col == tile).astype(I32), axis=0, keepdims=True)
    sched[0:1, :] = jnp.sum(hot * sub, axis=0, keepdims=True)
    sched[1:2, :] = jnp.sum(hot * in_col, axis=0, keepdims=True)
    sched[2:3, :] = jnp.sum(hot * (ties > 0).astype(I32), axis=0, keepdims=True)
    sched[3:4, :] = jnp.where(here > 0, upto - 1, SLOTS)


def kernel(
    t2_ref, tiles_ref, outs_ref, ins_ref, count_ref, out_ref,
    rows, stage, tiles, halves, meta, sched, plan, sums, acc, rx, zbuf, zrx, total, fin,
    swap_send, swap_recv, local_sem, plan_sem,
    zg_send, zg_recv, p1_send, p1_recv, p2_send, p2_recv, rx_send, rx_recv, zr_send, zr_recv,
):
    pair = lax.axis_index("pair")
    virt = lax.axis_index("virt")
    x, z = pair // NZ, pair % NZ
    y, c = virt // 2, virt % 2

    def at_z(d):
        return {"pair": x * NZ + (z + d + NZ) % NZ, "virt": virt}

    def at_x(d):
        return {"pair": (x + d) % NX * NZ + z, "virt": virt}

    def at_y(d):
        return {"pair": pair, "virt": (y + d) % NY * 2 + c}

    mate = {"pair": pair, "virt": y * 2 + 1 - c}

    def copy(src, dst, send, recv, device):
        return pltpu.make_async_remote_copy(
            src_ref=src, dst_ref=dst, send_sem=send, recv_sem=recv, device_id=device, device_id_type=MESH
        )

    sent = []

    def start(*what):
        one = copy(*what)
        one.start()
        sent.append(one)

    def arrived(ref, send, recv):
        copy(ref, ref, send, recv, mate).wait_recv()

    barrier = pltpu.get_barrier_semaphore()
    peers = [mate] + [at_z(d) for k in (4, 3, 2, 1) for d in (k, -k)]
    peers += [at_x(d) for d in (2, 1, 3)] + [at_y(d) for d in (2, 1, 3)]
    for peer in peers:
        pl.semaphore_signal(barrier, inc=1, device_id=peer, device_id_type=MESH)

    for row in range(4):
        for j in range(8):
            at = (row % 2) * 8 + j
            rows[row // 2, at : at + 1, :] = t2_ref[row : row + 1, j * W : (j + 1) * W]
    stage[c, 0, 0, 0] = rows[c]
    local = pltpu.make_async_copy(tiles_ref, tiles.at[pl.ds(c * LIST, LIST)], local_sem)
    local.start()
    lane = lax.broadcasted_iota(I32, (1, W), 1)
    pad = jnp.zeros((1, W - LIST), I32)
    key = jnp.concatenate([outs_ref[0] - y * 16, pad], axis=1) - c * 8
    key = jnp.where(lane < count_ref[0:1, 0:1], key, 8) + c * 9
    meta[c, 0:1, :] = key
    meta[c, 1:2, :] = jnp.concatenate([ins_ref[0], pad], axis=1)
    sums[SLOTS] = jnp.zeros((W, W), F32)
    pl.semaphore_wait(barrier, len(peers))

    start(rows.at[1 - c], stage.at[c, 0, 0, 0], swap_send.at[0], swap_recv.at[0], mate)
    start(meta.at[c], meta.at[c], swap_send.at[1], swap_recv.at[1], mate)
    arrived(stage.at[1 - c, 0, 0, 0], swap_send.at[0], swap_recv.at[0])

    def z_chunk(slot):
        return stage.at[:, 0, 0, slot]

    def z_start(slot, d):
        at = SLOT_OF[DELTAS[slot] - d]
        start(z_chunk(slot), z_chunk(at), zg_send.at[at], zg_recv.at[at], at_z(d))

    def z_arrived(slot):
        arrived(z_chunk(slot), zg_send.at[slot], zg_recv.at[slot])

    for k in (4, 3, 2, 1):
        z_start(0, k)
        z_start(0, -k)
    start(tiles_ref, tiles.at[pl.ds(c * LIST, LIST)], swap_send.at[2], swap_recv.at[2], mate)
    for k in (1, 2, 3, 4):
        z_arrived(SLOT_OF[-k])
        z_start(SLOT_OF[-k], 4)
        z_arrived(SLOT_OF[k])
        if k < 4:
            z_start(SLOT_OF[k], -4)

    def first_at(h, g, at):
        a, b = GROUPS[g]
        return stage.at[0, 0, at, pl.ds(a, b - a)] if h == 0 else stage.at[1, at, 0, pl.ds(a, b - a)]

    def first_start(g):
        for d in (2, 1, 3):
            for h in range(2):
                sems = p1_send.at[h, g, d - 1], p1_recv.at[h, g, d - 1]
                start(first_at(h, g, 0), first_at(h, g, 4 - d), *sems, (at_x, at_y)[h](d))

    def first_arrived(g):
        for d in (1, 3, 2):
            for h in range(2):
                arrived(first_at(h, g, 4 - d), p1_send.at[h, g, d - 1], p1_recv.at[h, g, d - 1])

    def second_at(h, g, at, part):
        a, b = GROUPS[g]
        if h == 0:
            return stage.at[0, at, pl.ds(2 * part, 2), pl.ds(a, b - a)]
        return stage.at[1, pl.ds(2 * part, 2), at, pl.ds(a, b - a)]

    MOVES = ((0, 0, 1), (0, 1, 3), (0, 1, 1), (0, 0, 3), (3, 0, 1), (1, 1, 3))

    def second_start(g, k):
        at, part, d = MOVES[k]
        for h in range(2):
            sems = p2_send.at[h, g, k], p2_recv.at[h, g, k]
            start(second_at(h, g, at, part), second_at(h, g, (at + 4 - d) % 4, part), *sems, (at_y, at_x)[h](d))

    def second_arrived(g, k):
        at, part, d = MOVES[k]
        for h in range(2):
            arrived(second_at(h, g, (at + 4 - d) % 4, part), p2_send.at[h, g, k], p2_recv.at[h, g, k])

    first_start(0)

    arrived(meta.at[1 - c], swap_send.at[1], swap_recv.at[1])
    low = lane < LIST
    both = [jnp.where(low, meta[0, k : k + 1, :], pltpu.roll(meta[1, k : k + 1, :], LIST, 1)) for k in range(2)]
    schedule(jnp.where(lane < SLOTS, both[0], 18), both[1], sched)
    turn = pltpu.make_async_copy(sched, plan, plan_sem)
    turn.start()
    local.wait()
    arrived(tiles.at[pl.ds((1 - c) * LIST, LIST)], swap_send.at[2], swap_recv.at[2])

    def halve(s, _):
        b = tiles[s]
        high = b.astype(BF)
        halves[s, :, :W] = high
        halves[s, :, W:] = (b - high.astype(F32)).astype(BF)
        return 0

    lax.fori_loop(0, SLOTS, halve, 0, unroll=4)
    turn.wait()

    first_arrived(0)
    for k in range(4):
        second_start(0, k)
    for k in (1, 2, 3, 4):
        z_arrived(SLOT_OF[-4 - k])
        if k < 4:
            z_arrived(SLOT_OF[4 + k])
    first_start(1)
    for k in (0, 1):
        second_arrived(0, k)
        second_start(0, 4 + k)
    first_arrived(1)
    for k in range(4):
        second_start(1, k)
    for k in range(2, 6):
        second_arrived(0, k)
    for k in (0, 1):
        second_arrived(1, k)
        second_start(1, 4 + k)
    for k in range(2, 6):
        second_arrived(1, k)

    flat = stage.reshape(2 * 4 * 4 * 16 * 16, W)

    def slot(k, running):
        n = plan[1, k]
        dy = (n // 16 + 4 - y) % 4
        a = flat[pl.ds((n // 8 % 2 * 4 + dy) * 1024 + n % 8, W, stride=8), :]
        keep = plan[2, k].astype(F32)
        high = a.astype(BF)
        a = jnp.concatenate([high, (a - high.astype(F32)).astype(BF)], axis=1)
        b = halves[plan[0, k]]
        product = jnp.dot(a, jnp.concatenate([b, b], axis=0), preferred_element_type=F32)
        running = running * keep + (product[:, :W] + product[:, W:])
        sums[k] = running
        return running

    def x_part(h, d):
        return acc.at[pl.ds(h * 8, 8), pl.ds(d * 32, 32), :]

    for h in range(2):
        lax.fori_loop(h * LIST, h * LIST + LIST, slot, jnp.zeros((W, W), F32), unroll=4)

        def pick(t, _):
            acc[t] = sums[plan[3, t]]
            return 0

        lax.fori_loop(h * 8, h * 8 + 8, pick, 0)
        for d in (2, 1, 3):
            start(x_part(h, d), rx.at[h, 3 - d], rx_send.at[h, 3 - d], rx_recv.at[h, 3 - d], at_x(d))

    acc_rows = acc.reshape(16 * W, W)
    rx_rows = rx.reshape(2 * 3 * 8 * 32, W)
    for h in range(2):
        for i in range(3):
            arrived(rx.at[h, i], rx_send.at[h, i], rx_recv.at[h, i])

        def add(s, _):
            for r in range(2):
                at = s * 2 + r
                value = acc_rows[pl.ds(h * 8 * W + at, 8, stride=W), :]
                for i in range(3):
                    value += rx_rows[pl.ds((h * 3 + i) * 256 + at, 8, stride=32), :]
                zbuf[h, s, r * 8 : r * 8 + 8, :] = value
            return 0

        lax.fori_loop(0, NZ, add, 0, unroll=2)
        for s in range(NZ - 1, 0, -1):
            back = SLOT_OF[-DELTAS[s]]
            start(zbuf.at[h, s], zrx.at[h, back], zr_send.at[h, back], zr_recv.at[h, back], at_z(DELTAS[s]))

    for h in range(2):
        value = zbuf[h, 0]
        for s in range(1, NZ):
            arrived(zrx.at[h, s], zr_send.at[h, s], zr_recv.at[h, s])
            value += zrx[h, s]
        total[h] = value

    fin[c] = total[c]
    start(total.at[1 - c], fin.at[c], swap_send.at[3], swap_recv.at[3], mate)
    arrived(fin.at[1 - c], swap_send.at[3], swap_recv.at[3])
    for row in range(4):
        for j in range(8):
            at = (row % 2) * 8 + j
            out_ref[row : row + 1, j * W : (j + 1) * W] = fin[row // 2, at : at + 1, :]

    for one in sent:
        one.wait_send()


def shards(t2_amplitudes, integral_tiles, out_tiles, in_tiles, tile_counts):
    vmem = pl.BlockSpec(memory_space=pltpu.VMEM)
    dma = pltpu.SemaphoreType.DMA
    return pl.pallas_call(
        kernel,
        out_shape=jax.ShapeDtypeStruct(t2_amplitudes.shape, F32),
        in_specs=[vmem, pl.BlockSpec(memory_space=pltpu.HBM), vmem, vmem, vmem],
        out_specs=vmem,
        scratch_shapes=[
            pltpu.VMEM((2, 16, W), F32),
            pltpu.VMEM((2, NY, NX, NZ, 16, W), F32),
            pltpu.VMEM((SLOTS, W, W), F32),
            pltpu.VMEM((SLOTS, W, 2 * W), BF),
            pltpu.VMEM((2, 8, W), I32),
            pltpu.VMEM((8, W), I32),
            pltpu.SMEM((8, W), I32),
            pltpu.VMEM((SLOTS + 1, W, W), F32),
            pltpu.VMEM((16, W, W), F32),
            pltpu.VMEM((2, 3, 8, 32, W), F32),
            pltpu.VMEM((2, NZ, 16, W), F32),
            pltpu.VMEM((2, NZ, 16, W), F32),
            pltpu.VMEM((2, 16, W), F32),
            pltpu.VMEM((2, 16, W), F32),
            dma((4,)), dma((4,)), dma, dma,
            dma((NZ,)), dma((NZ,)), dma((2, 2, 3)), dma((2, 2, 3)), dma((2, 2, 6)), dma((2, 2, 6)),
            dma((2, 3)), dma((2, 3)), dma((2, NZ)), dma((2, NZ)),
        ],
        compiler_params=pltpu.CompilerParams(
            collective_id=0, has_side_effects=True, vmem_limit_bytes=62 * 1024 * 1024
        ),
    )(t2_amplitudes, integral_tiles.reshape(LIST, W, W), out_tiles, in_tiles, tile_counts)


def solution(mesh):
    return jax.shard_map(
        shards,
        mesh=mesh,
        in_specs=(
            P("pair", "virt"),
            P("pair", "virt", None, None, None),
            P("pair", "virt", None),
            P("pair", "virt", None),
            P("pair", "virt"),
        ),
        out_specs=P("pair", "virt"),
        check_vma=False,
    )
```

```python
import jax
import jax.numpy as jnp
from jax import lax
from jax.experimental import pallas as pl
from jax.experimental.pallas import tpu as pltpu
from jax.sharding import PartitionSpec as P

W = 128
LIST = 32
NX = 4
NY = 4
NZ = 16
SLOTS = 2 * LIST
MESH = pl.DeviceIdType.MESH
F32 = jnp.float32
I32 = jnp.int32
BF = jnp.bfloat16
DELTAS = (0, 1, -1, 2, -2, 3, -3, 4, -4, 5, -5, 6, -6, 7, -7, 8)
SLOT_OF = {d: i for i, d in enumerate(DELTAS)}
SLOT_OF[-8] = SLOT_OF[8]
GROUPS = ((0, 1), (3, 5), (5, 8), (8, 13), (13, 16))
NG = len(GROUPS)


def schedule(key_row, in_row, sched):
    lane = lax.broadcasted_iota(I32, (W, W), 1)
    sub = lax.broadcasted_iota(I32, (W, W), 0)
    eye = lane == sub
    keys = jnp.broadcast_to(key_row, (W, W))
    key_col = jnp.sum(jnp.where(eye, keys, 0), axis=1, keepdims=True)
    in_col = jnp.sum(jnp.where(eye, jnp.broadcast_to(in_row, (W, W)), 0), axis=1, keepdims=True)
    below = jnp.sum((keys < key_col).astype(I32), axis=1, keepdims=True)
    ties = jnp.sum(((keys == key_col) & (lane < sub)).astype(I32), axis=1, keepdims=True)
    hot = ((below + ties) == lane).astype(I32)
    tile = lane + lane // 8
    upto = jnp.sum((key_col <= tile).astype(I32), axis=0, keepdims=True)
    here = jnp.sum((key_col == tile).astype(I32), axis=0, keepdims=True)
    sched[0:1, :] = jnp.sum(hot * sub, axis=0, keepdims=True)
    sched[1:2, :] = jnp.sum(hot * in_col, axis=0, keepdims=True)
    sched[2:3, :] = jnp.sum(hot * (ties > 0).astype(I32), axis=0, keepdims=True)
    sched[3:4, :] = jnp.where(here > 0, upto - 1, SLOTS)


def kernel(
    t2_hbm, tiles_ref, outs_hbm, ins_hbm, count_ref, out_ref,
    t2_ref, outs_ref, ins_ref, rows, stage_a, stage_b, tiles, halves, meta, sched, plan, sums, acc, rx, zbuf, zrx, total, fin,
    swap_send, swap_recv, local_sem, plan_sem, in_sem,
    zg_send, zg_recv, zw_send, zw_recv, p1_send, p1_recv, p2_send, p2_recv, rx_send, rx_recv, zr_send, zr_recv,
):
    pair = lax.axis_index("pair")
    virt = lax.axis_index("virt")
    x, z = pair // NZ, pair % NZ
    y, c = virt // 2, virt % 2

    def at_z(d, other=0):
        return {"pair": x * NZ + (z + d + NZ) % NZ, "virt": y * 2 + (1 - c if other else c)}

    def at_x(d):
        return {"pair": (x + d) % NX * NZ + z, "virt": virt}

    def at_y(d):
        return {"pair": pair, "virt": (y + d) % NY * 2 + c}

    mate = {"pair": pair, "virt": y * 2 + 1 - c}

    def stage(s):
        return (stage_a, stage_b)[s // 8], s % 8

    def copy(src, dst, send, recv, device):
        return pltpu.make_async_remote_copy(
            src_ref=src, dst_ref=dst, send_sem=send, recv_sem=recv, device_id=device, device_id_type=MESH
        )

    sent = []

    def start(*what):
        one = copy(*what)
        one.start()
        sent.append(one)

    def arrived(ref, send, recv):
        copy(ref, ref, send, recv, mate).wait_recv()

    barrier = pltpu.get_barrier_semaphore()
    peers = [mate] + [at_z(d, other) for d in (2, -2, 1, -1) for other in (0, 1)]
    peers += [at_x(d) for d in (2, 1, 3)] + [at_y(d) for d in (2, 1, 3)]
    for peer in peers:
        pl.semaphore_signal(barrier, inc=1, device_id=peer, device_id_type=MESH)

    fetches = [
        pltpu.make_async_copy(source, target, in_sem.at[i])
        for i, (source, target) in enumerate(
            ((t2_hbm, t2_ref), (outs_hbm, outs_ref), (ins_hbm, ins_ref))
        )
    ]
    for one in fetches:
        one.start()
    local = pltpu.make_async_copy(tiles_ref, tiles.at[pl.ds(c * LIST, LIST)], local_sem)
    local.start()
    sums[SLOTS] = jnp.zeros((64, W), F32)
    for one in fetches:
        one.wait()

    for row in range(4):
        for j in range(8):
            at = (row % 2) * 8 + j
            rows[row // 2, at : at + 1, :] = t2_ref[row : row + 1, j * W : (j + 1) * W]
    stage_a[c, 0, 0, 0] = rows[c]
    lane = lax.broadcasted_iota(I32, (1, W), 1)
    pad = jnp.zeros((1, W - LIST), I32)
    key = jnp.concatenate([outs_ref[0] - y * 16, pad], axis=1) - c * 8
    key = jnp.where(lane < count_ref[0:1, 0:1], key, 8) + c * 9
    meta[c, 0:1, :] = key
    meta[c, 1:2, :] = jnp.concatenate([ins_ref[0], pad], axis=1)
    pl.semaphore_wait(barrier, len(peers))

    start(rows.at[1 - c], stage_a.at[c, 0, 0, 0], zg_send.at[0, 1], zg_recv.at[0, 1], mate)
    for d in (1, -1, 2, -2):
        at = SLOT_OF[-d]
        for other in (0, 1):
            part = rows.at[1 - c if other else c]
            start(part, stage_a.at[c, 0, 0, at], zg_send.at[at, other], zg_recv.at[at, other], at_z(d, other))
    start(meta.at[c], meta.at[c], swap_send.at[1], swap_recv.at[1], mate)

    def z_near(slot):
        if slot > 0:
            arrived(stage_a.at[c, 0, 0, slot], zg_send.at[slot, 0], zg_recv.at[slot, 0])
        arrived(stage_a.at[1 - c, 0, 0, slot], zg_send.at[slot, 1], zg_recv.at[slot, 1])

    def z_chunk(slot):
        ref, at = stage(slot)
        return ref.at[:, 0, 0, at]

    def z_pass(slot, d):
        at = SLOT_OF[DELTAS[slot] - d]
        start(z_chunk(slot), z_chunk(at), zg_send.at[at, 0], zg_recv.at[at, 0], at_z(d))

    def z_far(k):
        for slot in (SLOT_OF[-k], SLOT_OF[k])[: 1 if k == 8 else 2]:
            arrived(z_chunk(slot), zg_send.at[slot, 0], zg_recv.at[slot, 0])

    def whole(slot, piece):
        return stage_a.at[:, 0, pl.ds(1, 3), slot] if piece == 2 else stage_a.at[piece, pl.ds(1, 3), :, slot]

    def whole_start():
        for piece in range(3):
            for d in (1, -1):
                at = SLOT_OF[-d]
                start(whole(0, piece), whole(at, piece), zw_send.at[at - 1, piece], zw_recv.at[at - 1, piece], at_z(d))

    def whole_arrived():
        for piece in range(3):
            for at in (1, 2):
                arrived(whole(at, piece), zw_send.at[at - 1, piece], zw_recv.at[at - 1, piece])

    def first_at(h, g, at):
        ref, a = stage(GROUPS[g][0])
        slots = pl.ds(a, GROUPS[g][1] - GROUPS[g][0])
        return ref.at[0, 0, at, slots] if h == 0 else ref.at[1, at, 0, slots]

    def first_start(g):
        for d in (2, 1, 3):
            for h in range(2):
                sems = p1_send.at[h, g, d - 1], p1_recv.at[h, g, d - 1]
                start(first_at(h, g, 0), first_at(h, g, 4 - d), *sems, (at_x, at_y)[h](d))

    def first_arrived(g):
        for d in (1, 3, 2):
            for h in range(2):
                arrived(first_at(h, g, 4 - d), p1_send.at[h, g, d - 1], p1_recv.at[h, g, d - 1])

    def second_at(h, g, at, part):
        ref, a = stage(GROUPS[g][0])
        slots = pl.ds(a, GROUPS[g][1] - GROUPS[g][0])
        if h == 0:
            return ref.at[0, at, pl.ds(2 * part, 2), slots]
        return ref.at[1, pl.ds(2 * part, 2), at, slots]

    MOVES = ((0, 0, 1), (0, 1, 3), (0, 1, 1), (0, 0, 3), (3, 0, 1), (1, 1, 3))

    def second_start(g, k):
        at, part, d = MOVES[k]
        for h in range(2):
            sems = p2_send.at[h, g, k], p2_recv.at[h, g, k]
            start(second_at(h, g, at, part), second_at(h, g, (at + 4 - d) % 4, part), *sems, (at_y, at_x)[h](d))

    def second_arrived(g, k):
        at, part, d = MOVES[k]
        for h in range(2):
            arrived(second_at(h, g, (at + 4 - d) % 4, part), p2_send.at[h, g, k], p2_recv.at[h, g, k])

    def second_open(g):
        first_arrived(g)
        for k in range(4):
            second_start(g, k)

    def second_pass(g):
        for k in (0, 1):
            second_arrived(g, k)
            second_start(g, 4 + k)

    def halve(s, _):
        b = tiles[s]
        high = b.astype(BF)
        halves[s, :, :W] = high
        halves[s, :, W:] = (b - high.astype(F32)).astype(BF)
        return 0

    def halve_some(i):
        lax.fori_loop(i * 16, i * 16 + 16, halve, 0, unroll=2)

    flats = [ref.reshape(2 * 4 * 4 * 8 * 16, W) for ref in (stage_a, stage_b)]
    acc_rows = acc.reshape(2 * 16 * 64, W)
    rx_rows = rx.reshape(2 * 2 * 3 * 8 * 16, W)

    def products(g, h):
        def slot(k, running):
            n = plan[1, k]
            dy = (n // 16 + 4 - y) % 4
            a = flats[g][pl.ds((n // 8 % 2 * 4 + dy) * 512 + n % 8, 64, stride=8), :]
            keep = plan[2, k].astype(F32)
            high = a.astype(BF)
            a = jnp.concatenate([high, (a - high.astype(F32)).astype(BF)], axis=1)
            b = halves[plan[0, k]]
            product = jnp.dot(a, jnp.concatenate([b, b], axis=0), preferred_element_type=F32)
            running = running * keep + (product[:, :W] + product[:, W:])
            sums[k] = running
            return running

        lax.fori_loop(h * LIST, h * LIST + LIST, slot, jnp.zeros((64, W), F32), unroll=4)

        def pick(t, _):
            acc[g, t] = sums[plan[3, t]]
            return 0

        lax.fori_loop(h * 8, h * 8 + 8, pick, 0)
        for d in (2, 1, 3):
            part = acc.at[g, pl.ds(h * 8, 8), pl.ds(d * 16, 16), :]
            start(part, rx.at[g, h, 3 - d], rx_send.at[g, h, 3 - d], rx_recv.at[g, h, 3 - d], at_x(d))

    def add_up(g, h):
        for i in range(3):
            arrived(rx.at[g, h, i], rx_send.at[g, h, i], rx_recv.at[g, h, i])

        def add(s, _):
            for r in range(2):
                at = s * 2 + r
                value = acc_rows[pl.ds((g * 16 + h * 8) * 64 + at, 8, stride=64), :]
                for i in range(3):
                    value += rx_rows[pl.ds(((g * 2 + h) * 3 + i) * 128 + at, 8, stride=16), :]
                zbuf[h, g * 8 + s, r * 8 : r * 8 + 8, :] = value
            return 0

        lax.fori_loop(0, 8, add, 0, unroll=2)
        for s in range(g * 8 + 7, max(g * 8 - 1, 0), -1):
            back = SLOT_OF[-DELTAS[s]]
            start(zbuf.at[h, s], zrx.at[h, back], zr_send.at[h, back], zr_recv.at[h, back], at_z(DELTAS[s]))

    z_near(0)
    first_start(0)
    start(tiles_ref, tiles.at[pl.ds(c * LIST, LIST)], swap_send.at[2], swap_recv.at[2], mate)
    for k in (1, -1):
        z_near(SLOT_OF[k])
        z_pass(SLOT_OF[k], -2 * k)
    for k in (2, -2):
        z_near(SLOT_OF[k])
        z_pass(SLOT_OF[k], -k)
    first_start(1)
    for k in (1, -1, 2, -2):
        z_pass(SLOT_OF[k], -4 if k > 0 else 4)
    second_open(0)

    arrived(meta.at[1 - c], swap_send.at[1], swap_recv.at[1])
    low = lane < LIST
    both = [jnp.where(low, meta[0, k : k + 1, :], pltpu.roll(meta[1, k : k + 1, :], LIST, 1)) for k in range(2)]
    schedule(jnp.where(lane < SLOTS, both[0], 18), both[1], sched)
    turn = pltpu.make_async_copy(sched, plan, plan_sem)
    turn.start()

    z_far(3)
    z_pass(SLOT_OF[3], -4)
    z_pass(SLOT_OF[-3], 4)
    z_far(4)
    z_pass(SLOT_OF[-4], 4)
    first_start(2)
    second_pass(0)
    second_open(1)
    for k in range(2, 6):
        second_arrived(0, k)
    whole_start()
    z_far(5)
    z_far(6)
    first_start(3)
    local.wait()
    arrived(tiles.at[pl.ds((1 - c) * LIST, LIST)], swap_send.at[2], swap_recv.at[2])
    halve_some(0)
    second_pass(1)
    second_open(2)
    halve_some(1)
    z_far(7)
    z_far(8)
    first_start(4)
    halve_some(2)
    second_open(3)
    halve_some(3)
    turn.wait()
    second_pass(2)
    second_open(4)
    whole_arrived()
    for g in (1, 2):
        for k in range(2, 6):
            second_arrived(g, k)
    products(0, 0)
    second_pass(3)
    products(0, 1)
    second_pass(4)
    add_up(0, 0)
    add_up(0, 1)
    for g in (3, 4):
        for k in range(2, 6):
            second_arrived(g, k)
    for h in range(2):
        products(1, h)
    for h in range(2):
        add_up(1, h)

    for h in range(2):
        value = zbuf[h, 0]
        for s in range(1, NZ):
            arrived(zrx.at[h, s], zr_send.at[h, s], zr_recv.at[h, s])
            value += zrx[h, s]
        total[h] = value

    fin[c] = total[c]
    start(total.at[1 - c], fin.at[c], swap_send.at[3], swap_recv.at[3], mate)
    arrived(fin.at[1 - c], swap_send.at[3], swap_recv.at[3])
    for row in range(4):
        for j in range(8):
            at = (row % 2) * 8 + j
            out_ref[row : row + 1, j * W : (j + 1) * W] = fin[row // 2, at : at + 1, :]

    for one in sent:
        one.wait_send()


def shards(t2_amplitudes, integral_tiles, out_tiles, in_tiles, tile_counts):
    vmem = pl.BlockSpec(memory_space=pltpu.VMEM)
    dma = pltpu.SemaphoreType.DMA
    return pl.pallas_call(
        kernel,
        out_shape=jax.ShapeDtypeStruct(t2_amplitudes.shape, F32),
        in_specs=[pl.BlockSpec(memory_space=pltpu.HBM)] * 4 + [vmem],
        out_specs=vmem,
        scratch_shapes=[
            pltpu.VMEM(t2_amplitudes.shape, F32),
            pltpu.VMEM(out_tiles.shape, I32),
            pltpu.VMEM(in_tiles.shape, I32),
            pltpu.VMEM((2, 16, W), F32),
            pltpu.VMEM((2, NY, NX, 8, 16, W), F32),
            pltpu.VMEM((2, NY, NX, 8, 16, W), F32),
            pltpu.VMEM((SLOTS, W, W), F32),
            pltpu.VMEM((SLOTS, W, 2 * W), BF),
            pltpu.VMEM((2, 8, W), I32),
            pltpu.VMEM((8, W), I32),
            pltpu.SMEM((8, W), I32),
            pltpu.VMEM((SLOTS + 1, 64, W), F32),
            pltpu.VMEM((2, 16, 64, W), F32),
            pltpu.VMEM((2, 2, 3, 8, 16, W), F32),
            pltpu.VMEM((2, NZ, 16, W), F32),
            pltpu.VMEM((2, NZ, 16, W), F32),
            pltpu.VMEM((2, 16, W), F32),
            pltpu.VMEM((2, 16, W), F32),
            dma((4,)), dma((4,)), dma, dma, dma((3,)),
            dma((NZ, 2)), dma((NZ, 2)), dma((2, 3)), dma((2, 3)), dma((2, NG, 3)), dma((2, NG, 3)), dma((2, NG, 6)), dma((2, NG, 6)),
            dma((2, 2, 3)), dma((2, 2, 3)), dma((2, NZ)), dma((2, NZ)),
        ],
        compiler_params=pltpu.CompilerParams(
            collective_id=0, has_side_effects=True, vmem_limit_bytes=62 * 1024 * 1024
        ),
    )(t2_amplitudes, integral_tiles.reshape(LIST, W, W), out_tiles, in_tiles, tile_counts)


def solution(mesh):
    return jax.shard_map(
        shards,
        mesh=mesh,
        in_specs=(
            P("pair", "virt"),
            P("pair", "virt", None, None, None),
            P("pair", "virt", None),
            P("pair", "virt", None),
            P("pair", "virt"),
        ),
        out_specs=P("pair", "virt"),
        check_vma=False,
    )
```

```python
import jax
import jax.numpy as jnp
from jax import lax
from jax.experimental import pallas as pl
from jax.experimental.pallas import tpu as pltpu
from jax.sharding import PartitionSpec as P

W = 128
LIST = 32
NX = 4
NY = 4
NZ = 16
SLOTS = 2 * LIST
MESH = pl.DeviceIdType.MESH
F32 = jnp.float32
I32 = jnp.int32
BF = jnp.bfloat16
DELTAS = (0, 1, -1, 2, -2, 7, -7, 8, 3, -3, 4, -4, 5, -5, 6, -6)
SLOT_OF = {d: i for i, d in enumerate(DELTAS)}
SLOT_OF[-8] = SLOT_OF[8]
GROUPS = ((0, 1), (3, 5), (5, 8), (8, 12), (12, 16))
NG = len(GROUPS)


def schedule(key_row, in_row, sched):
    lane = lax.broadcasted_iota(I32, (W, W), 1)
    sub = lax.broadcasted_iota(I32, (W, W), 0)
    eye = lane == sub
    keys = jnp.broadcast_to(key_row, (W, W))
    key_col = jnp.sum(jnp.where(eye, keys, 0), axis=1, keepdims=True)
    in_col = jnp.sum(jnp.where(eye, jnp.broadcast_to(in_row, (W, W)), 0), axis=1, keepdims=True)
    below = jnp.sum((keys < key_col).astype(I32), axis=1, keepdims=True)
    ties = jnp.sum(((keys == key_col) & (lane < sub)).astype(I32), axis=1, keepdims=True)
    hot = ((below + ties) == lane).astype(I32)
    tile = lane + lane // 8
    upto = jnp.sum((key_col <= tile).astype(I32), axis=0, keepdims=True)
    here = jnp.sum((key_col == tile).astype(I32), axis=0, keepdims=True)
    sched[0:1, :] = jnp.sum(hot * sub, axis=0, keepdims=True)
    sched[1:2, :] = jnp.sum(hot * in_col, axis=0, keepdims=True)
    sched[2:3, :] = jnp.sum(hot * (ties > 0).astype(I32), axis=0, keepdims=True)
    sched[3:4, :] = jnp.where(here > 0, upto - 1, SLOTS)


def kernel(
    t2_hbm, tiles_ref, outs_hbm, ins_hbm, count_ref, out_ref,
    t2_ref, outs_ref, ins_ref, rows, stage_a, stage_b, tiles, halves, meta, sched, plan, sums, acc, rx, zbuf, zrx, total, fin,
    swap_send, swap_recv, local_sem, plan_sem, in_sem,
    zg_send, zg_recv, zw_send, zw_recv, p1_send, p1_recv, p2_send, p2_recv, rx_send, rx_recv, zr_send, zr_recv,
):
    pair = lax.axis_index("pair")
    virt = lax.axis_index("virt")
    x, z = pair // NZ, pair % NZ
    y, c = virt // 2, virt % 2

    def at_z(d, other=0):
        return {"pair": x * NZ + (z + d + NZ) % NZ, "virt": y * 2 + (1 - c if other else c)}

    def at_x(d):
        return {"pair": (x + d) % NX * NZ + z, "virt": virt}

    def at_y(d):
        return {"pair": pair, "virt": (y + d) % NY * 2 + c}

    mate = {"pair": pair, "virt": y * 2 + 1 - c}

    def stage(s):
        return (stage_a, stage_b)[s // 8], s % 8

    def copy(src, dst, send, recv, device):
        return pltpu.make_async_remote_copy(
            src_ref=src, dst_ref=dst, send_sem=send, recv_sem=recv, device_id=device, device_id_type=MESH
        )

    sent = []

    def start(*what):
        one = copy(*what)
        one.start()
        sent.append(one)

    def arrived(ref, send, recv):
        copy(ref, ref, send, recv, mate).wait_recv()

    barrier = pltpu.get_barrier_semaphore()
    peers = [mate] + [at_z(d, other) for d in (2, -2, 1, -1) for other in (0, 1)]
    peers += [at_x(d) for d in (2, 1, 3)] + [at_y(d) for d in (2, 1, 3)]
    for peer in peers:
        pl.semaphore_signal(barrier, inc=1, device_id=peer, device_id_type=MESH)

    fetches = [
        pltpu.make_async_copy(source, target, in_sem.at[i])
        for i, (source, target) in enumerate(
            ((t2_hbm, t2_ref), (outs_hbm, outs_ref), (ins_hbm, ins_ref))
        )
    ]
    for one in fetches:
        one.start()
    local = pltpu.make_async_copy(tiles_ref, tiles.at[pl.ds(c * LIST, LIST)], local_sem)
    local.start()
    sums[SLOTS] = jnp.zeros((64, W), F32)
    for one in fetches:
        one.wait()

    for row in range(4):
        for j in range(8):
            at = (row % 2) * 8 + j
            rows[row // 2, at : at + 1, :] = t2_ref[row : row + 1, j * W : (j + 1) * W]
    stage_a[c, 0, 0, 0] = rows[c]
    lane = lax.broadcasted_iota(I32, (1, W), 1)
    pad = jnp.zeros((1, W - LIST), I32)
    key = jnp.concatenate([outs_ref[0] - y * 16, pad], axis=1) - c * 8
    key = jnp.where(lane < count_ref[0:1, 0:1], key, 8) + c * 9
    meta[c, 0:1, :] = key
    meta[c, 1:2, :] = jnp.concatenate([ins_ref[0], pad], axis=1)
    pl.semaphore_wait(barrier, len(peers))

    start(rows.at[1 - c], stage_a.at[c, 0, 0, 0], zg_send.at[0, 1], zg_recv.at[0, 1], mate)
    for d in (1, -1, 2, -2):
        at = SLOT_OF[-d]
        for other in (0, 1):
            part = rows.at[1 - c if other else c]
            ref, slot = stage(at)
            start(part, ref.at[c, 0, 0, slot], zg_send.at[at, other], zg_recv.at[at, other], at_z(d, other))
    start(meta.at[c], meta.at[c], swap_send.at[1], swap_recv.at[1], mate)

    def z_near(slot):
        ref, at = stage(slot)
        if slot > 0:
            arrived(ref.at[c, 0, 0, at], zg_send.at[slot, 0], zg_recv.at[slot, 0])
        arrived(ref.at[1 - c, 0, 0, at], zg_send.at[slot, 1], zg_recv.at[slot, 1])

    def z_chunk(slot):
        ref, at = stage(slot)
        return ref.at[:, 0, 0, at]

    def z_pass(slot, d):
        at = SLOT_OF[DELTAS[slot] - d]
        start(z_chunk(slot), z_chunk(at), zg_send.at[at, 0], zg_recv.at[at, 0], at_z(d))

    def z_far(k):
        for slot in (SLOT_OF[-k], SLOT_OF[k])[: 1 if k == 8 else 2]:
            arrived(z_chunk(slot), zg_send.at[slot, 0], zg_recv.at[slot, 0])

    def whole(slot, piece):
        return stage_a.at[:, 0, pl.ds(1, 3), slot] if piece == 2 else stage_a.at[piece, pl.ds(1, 3), :, slot]

    def whole_start():
        for piece in range(3):
            for d in (1, -1):
                at = SLOT_OF[-d]
                start(whole(0, piece), whole(at, piece), zw_send.at[at - 1, piece], zw_recv.at[at - 1, piece], at_z(d))

    def whole_arrived():
        for piece in range(3):
            for at in (1, 2):
                arrived(whole(at, piece), zw_send.at[at - 1, piece], zw_recv.at[at - 1, piece])

    def first_at(h, g, at):
        ref, a = stage(GROUPS[g][0])
        slots = pl.ds(a, GROUPS[g][1] - GROUPS[g][0])
        return ref.at[0, 0, at, slots] if h == 0 else ref.at[1, at, 0, slots]

    def first_start(g):
        for d in (2, 1, 3):
            for h in range(2):
                sems = p1_send.at[h, g, d - 1], p1_recv.at[h, g, d - 1]
                start(first_at(h, g, 0), first_at(h, g, 4 - d), *sems, (at_x, at_y)[h](d))

    def first_arrived(g):
        for d in (1, 3, 2):
            for h in range(2):
                arrived(first_at(h, g, 4 - d), p1_send.at[h, g, d - 1], p1_recv.at[h, g, d - 1])

    def second_at(h, g, at, part):
        ref, a = stage(GROUPS[g][0])
        slots = pl.ds(a, GROUPS[g][1] - GROUPS[g][0])
        if h == 0:
            return ref.at[0, at, pl.ds(2 * part, 2), slots]
        return ref.at[1, pl.ds(2 * part, 2), at, slots]

    MOVES = ((0, 0, 1), (0, 1, 3), (0, 1, 1), (0, 0, 3), (3, 0, 1), (1, 1, 3))

    def second_start(g, k):
        at, part, d = MOVES[k]
        for h in range(2):
            sems = p2_send.at[h, g, k], p2_recv.at[h, g, k]
            start(second_at(h, g, at, part), second_at(h, g, (at + 4 - d) % 4, part), *sems, (at_y, at_x)[h](d))

    def second_arrived(g, k):
        at, part, d = MOVES[k]
        for h in range(2):
            arrived(second_at(h, g, (at + 4 - d) % 4, part), p2_send.at[h, g, k], p2_recv.at[h, g, k])

    def second_open(g):
        first_arrived(g)
        for k in range(4):
            second_start(g, k)

    def second_pass(g):
        for k in (0, 1):
            second_arrived(g, k)
            second_start(g, 4 + k)

    def halve(s, _):
        b = tiles[s]
        high = b.astype(BF)
        halves[s, :, :W] = high
        halves[s, :, W:] = (b - high.astype(F32)).astype(BF)
        return 0

    def halve_some(i):
        lax.fori_loop(i * 16, i * 16 + 16, halve, 0, unroll=2)

    flats = [ref.reshape(2 * 4 * 4 * 8 * 16, W) for ref in (stage_a, stage_b)]
    acc_rows = acc.reshape(2 * 16 * 64, W)
    rx_rows = rx.reshape(2 * 2 * 3 * 8 * 16, W)

    def products(g, h):
        def slot(k, running):
            n = plan[1, k]
            dy = (n // 16 + 4 - y) % 4
            a = flats[g][pl.ds((n // 8 % 2 * 4 + dy) * 512 + n % 8, 64, stride=8), :]
            keep = plan[2, k].astype(F32)
            high = a.astype(BF)
            a = jnp.concatenate([high, (a - high.astype(F32)).astype(BF)], axis=1)
            b = halves[plan[0, k]]
            product = jnp.dot(a, jnp.concatenate([b, b], axis=0), preferred_element_type=F32)
            running = running * keep + (product[:, :W] + product[:, W:])
            sums[k] = running
            return running

        lax.fori_loop(h * LIST, h * LIST + LIST, slot, jnp.zeros((64, W), F32), unroll=8)

        def pick(t, _):
            acc[g, t] = sums[plan[3, t]]
            return 0

        lax.fori_loop(h * 8, h * 8 + 8, pick, 0)
        for d in (2, 1, 3):
            part = acc.at[g, pl.ds(h * 8, 8), pl.ds(d * 16, 16), :]
            start(part, rx.at[g, h, 3 - d], rx_send.at[g, h, 3 - d], rx_recv.at[g, h, 3 - d], at_x(d))

    def add_up(g, h):
        for i in range(3):
            arrived(rx.at[g, h, i], rx_send.at[g, h, i], rx_recv.at[g, h, i])

        def add(s, _):
            for r in range(2):
                at = s * 2 + r
                value = acc_rows[pl.ds((g * 16 + h * 8) * 64 + at, 8, stride=64), :]
                for i in range(3):
                    value += rx_rows[pl.ds(((g * 2 + h) * 3 + i) * 128 + at, 8, stride=16), :]
                zbuf[h, g * 8 + s, r * 8 : r * 8 + 8, :] = value
            return 0

        lax.fori_loop(0, 8, add, 0, unroll=2)
        for s in sorted(range(max(g * 8, 1), g * 8 + 8), key=lambda s: -abs(DELTAS[s])):
            back = SLOT_OF[-DELTAS[s]]
            start(zbuf.at[h, s], zrx.at[h, back], zr_send.at[h, back], zr_recv.at[h, back], at_z(DELTAS[s]))

    z_near(0)
    first_start(0)
    start(tiles_ref, tiles.at[pl.ds(c * LIST, LIST)], swap_send.at[2], swap_recv.at[2], mate)
    for k in (1, -1):
        z_near(SLOT_OF[k])
        z_pass(SLOT_OF[k], -2 * k)
    for k in (2, -2):
        z_near(SLOT_OF[k])
        z_pass(SLOT_OF[k], -k)
    first_start(1)
    for k in (1, -1, 2, -2):
        z_pass(SLOT_OF[k], -4 if k > 0 else 4)
    second_open(0)

    arrived(meta.at[1 - c], swap_send.at[1], swap_recv.at[1])
    low = lane < LIST
    both = [jnp.where(low, meta[0, k : k + 1, :], pltpu.roll(meta[1, k : k + 1, :], LIST, 1)) for k in range(2)]
    schedule(jnp.where(lane < SLOTS, both[0], 18), both[1], sched)
    turn = pltpu.make_async_copy(sched, plan, plan_sem)
    turn.start()

    z_far(3)
    z_pass(SLOT_OF[3], -4)
    z_pass(SLOT_OF[-3], 4)
    z_far(4)
    z_pass(SLOT_OF[-4], 4)
    first_start(3)
    second_pass(0)
    second_open(1)
    for k in range(2, 6):
        second_arrived(0, k)
    whole_start()
    z_far(5)
    z_far(6)
    first_start(4)
    local.wait()
    arrived(tiles.at[pl.ds((1 - c) * LIST, LIST)], swap_send.at[2], swap_recv.at[2])
    halve_some(0)
    second_pass(1)
    second_open(3)
    halve_some(1)
    z_far(7)
    z_far(8)
    first_start(2)
    halve_some(2)
    second_open(4)
    halve_some(3)
    second_pass(3)
    second_open(2)
    turn.wait()
    second_pass(4)
    for g in (3, 4):
        for k in range(2, 6):
            second_arrived(g, k)
    second_pass(2)
    products(1, 0)
    products(1, 1)
    whole_arrived()
    for g in (1, 2):
        for k in range(2, 6):
            second_arrived(g, k)
    products(0, 0)
    add_up(1, 0)
    products(0, 1)
    add_up(1, 1)
    for h in range(2):
        add_up(0, h)

    for h in range(2):
        value = zbuf[h, 0]
        for s in range(1, NZ):
            arrived(zrx.at[h, s], zr_send.at[h, s], zr_recv.at[h, s])
            value += zrx[h, s]
        total[h] = value

    fin[c] = total[c]
    start(total.at[1 - c], fin.at[c], swap_send.at[3], swap_recv.at[3], mate)
    arrived(fin.at[1 - c], swap_send.at[3], swap_recv.at[3])
    for row in range(4):
        for j in range(8):
            at = (row % 2) * 8 + j
            out_ref[row : row + 1, j * W : (j + 1) * W] = fin[row // 2, at : at + 1, :]

    for one in sent:
        one.wait_send()


def shards(t2_amplitudes, integral_tiles, out_tiles, in_tiles, tile_counts):
    vmem = pl.BlockSpec(memory_space=pltpu.VMEM)
    dma = pltpu.SemaphoreType.DMA
    return pl.pallas_call(
        kernel,
        out_shape=jax.ShapeDtypeStruct(t2_amplitudes.shape, F32),
        in_specs=[pl.BlockSpec(memory_space=pltpu.HBM)] * 4 + [vmem],
        out_specs=vmem,
        scratch_shapes=[
            pltpu.VMEM(t2_amplitudes.shape, F32),
            pltpu.VMEM(out_tiles.shape, I32),
            pltpu.VMEM(in_tiles.shape, I32),
            pltpu.VMEM((2, 16, W), F32),
            pltpu.VMEM((2, NY, NX, 8, 16, W), F32),
            pltpu.VMEM((2, NY, NX, 8, 16, W), F32),
            pltpu.VMEM((SLOTS, W, W), F32),
            pltpu.VMEM((SLOTS, W, 2 * W), BF),
            pltpu.VMEM((2, 8, W), I32),
            pltpu.VMEM((8, W), I32),
            pltpu.SMEM((8, W), I32),
            pltpu.VMEM((SLOTS + 1, 64, W), F32),
            pltpu.VMEM((2, 16, 64, W), F32),
            pltpu.VMEM((2, 2, 3, 8, 16, W), F32),
            pltpu.VMEM((2, NZ, 16, W), F32),
            pltpu.VMEM((2, NZ, 16, W), F32),
            pltpu.VMEM((2, 16, W), F32),
            pltpu.VMEM((2, 16, W), F32),
            dma((4,)), dma((4,)), dma, dma, dma((3,)),
            dma((NZ, 2)), dma((NZ, 2)), dma((2, 3)), dma((2, 3)), dma((2, NG, 3)), dma((2, NG, 3)), dma((2, NG, 6)), dma((2, NG, 6)),
            dma((2, 2, 3)), dma((2, 2, 3)), dma((2, NZ)), dma((2, NZ)),
        ],
        compiler_params=pltpu.CompilerParams(
            collective_id=0, has_side_effects=True, vmem_limit_bytes=62 * 1024 * 1024
        ),
    )(t2_amplitudes, integral_tiles.reshape(LIST, W, W), out_tiles, in_tiles, tile_counts)


def solution(mesh):
    return jax.shard_map(
        shards,
        mesh=mesh,
        in_specs=(
            P("pair", "virt"),
            P("pair", "virt", None, None, None),
            P("pair", "virt", None),
            P("pair", "virt", None),
            P("pair", "virt"),
        ),
        out_specs=P("pair", "virt"),
        check_vma=False,
    )
```

```python
import jax
import jax.numpy as jnp
from jax import lax
from jax.experimental import pallas as pl
from jax.experimental.pallas import tpu as pltpu
from jax.sharding import PartitionSpec as P

W = 128
LIST = 32
NX = 4
NY = 4
NZ = 16
SLOTS = 2 * LIST
MESH = pl.DeviceIdType.MESH
F32 = jnp.float32
I32 = jnp.int32
BF = jnp.bfloat16
DELTAS = (0, 1, -1, 2, -2, 7, -7, 8, 3, -3, 4, -4, 5, -5, 6, -6)
SLOT_OF = {d: i for i, d in enumerate(DELTAS)}
SLOT_OF[-8] = SLOT_OF[8]
GROUPS = ((0, 1), (3, 5), (5, 8), (8, 12), (12, 16))
NG = len(GROUPS)


def schedule(key_row, in_row, sched):
    lane = lax.broadcasted_iota(I32, (W, W), 1)
    sub = lax.broadcasted_iota(I32, (W, W), 0)
    eye = lane == sub
    keys = jnp.broadcast_to(key_row, (W, W))
    key_col = jnp.sum(jnp.where(eye, keys, 0), axis=1, keepdims=True)
    in_col = jnp.sum(jnp.where(eye, jnp.broadcast_to(in_row, (W, W)), 0), axis=1, keepdims=True)
    below = jnp.sum((keys < key_col).astype(I32), axis=1, keepdims=True)
    ties = jnp.sum(((keys == key_col) & (lane < sub)).astype(I32), axis=1, keepdims=True)
    hot = ((below + ties) == lane).astype(I32)
    tile = lane + lane // 8
    upto = jnp.sum((key_col <= tile).astype(I32), axis=0, keepdims=True)
    here = jnp.sum((key_col == tile).astype(I32), axis=0, keepdims=True)
    sched[0:1, :] = jnp.sum(hot * sub, axis=0, keepdims=True)
    sched[1:2, :] = jnp.sum(hot * in_col, axis=0, keepdims=True)
    sched[2:3, :] = jnp.sum(hot * (ties > 0).astype(I32), axis=0, keepdims=True)
    sched[3:4, :] = jnp.where(here > 0, upto - 1, SLOTS)


def kernel(
    t2_hbm, tiles_ref, outs_hbm, ins_hbm, count_ref, out_ref,
    t2_ref, outs_ref, ins_ref, rows, stage_a, stage_b, tiles, halves, meta, sched, plan, sums, acc, rx, zbuf, zrx, fin,
    swap_send, swap_recv, local_sem, plan_sem, in_sem,
    zg_send, zg_recv, zw_send, zw_recv, p1_send, p1_recv, p2_send, p2_recv, rx_send, rx_recv, zr_send, zr_recv,
):
    pair = lax.axis_index("pair")
    virt = lax.axis_index("virt")
    x, z = pair // NZ, pair % NZ
    y, c = virt // 2, virt % 2

    def at_z(d, other=0):
        return {"pair": x * NZ + (z + d + NZ) % NZ, "virt": y * 2 + (1 - c if other else c)}

    def at_x(d):
        return {"pair": (x + d) % NX * NZ + z, "virt": virt}

    def at_y(d):
        return {"pair": pair, "virt": (y + d) % NY * 2 + c}

    mate = {"pair": pair, "virt": y * 2 + 1 - c}

    def stage(s):
        return (stage_a, stage_b)[s // 8], s % 8

    def copy(src, dst, send, recv, device):
        return pltpu.make_async_remote_copy(
            src_ref=src, dst_ref=dst, send_sem=send, recv_sem=recv, device_id=device, device_id_type=MESH
        )

    sent = []

    def start(*what):
        one = copy(*what)
        one.start()
        sent.append(one)

    def arrived(ref, send, recv):
        copy(ref, ref, send, recv, mate).wait_recv()

    barrier = pltpu.get_barrier_semaphore()
    peers = [mate] + [at_z(d, other) for d in (2, -2, 1, -1) for other in (0, 1)]
    peers += [at_x(d) for d in (2, 1, 3)] + [at_y(d) for d in (2, 1, 3)]
    for peer in peers:
        pl.semaphore_signal(barrier, inc=1, device_id=peer, device_id_type=MESH)

    fetches = [
        pltpu.make_async_copy(source, target, in_sem.at[i])
        for i, (source, target) in enumerate(
            ((t2_hbm, t2_ref), (outs_hbm, outs_ref), (ins_hbm, ins_ref))
        )
    ]
    for one in fetches:
        one.start()
    local = pltpu.make_async_copy(tiles_ref, tiles.at[pl.ds(c * LIST, LIST)], local_sem)
    local.start()
    sums[SLOTS] = jnp.zeros((64, W), F32)
    for one in fetches:
        one.wait()

    for row in range(4):
        for j in range(8):
            at = (row % 2) * 8 + j
            rows[row // 2, at : at + 1, :] = t2_ref[row : row + 1, j * W : (j + 1) * W]
    stage_a[c, 0, 0, 0] = rows[c]
    lane = lax.broadcasted_iota(I32, (1, W), 1)
    pad = jnp.zeros((1, W - LIST), I32)
    key = jnp.concatenate([outs_ref[0] - y * 16, pad], axis=1) - c * 8
    key = jnp.where(lane < count_ref[0:1, 0:1], key, 8) + c * 9
    meta[c, 0:1, :] = key
    meta[c, 1:2, :] = jnp.concatenate([ins_ref[0], pad], axis=1)
    pl.semaphore_wait(barrier, len(peers))

    start(rows.at[1 - c], stage_a.at[c, 0, 0, 0], zg_send.at[0, 1], zg_recv.at[0, 1], mate)
    for d in (1, -1, 2, -2):
        at = SLOT_OF[-d]
        for other in (0, 1):
            part = rows.at[1 - c if other else c]
            ref, slot = stage(at)
            start(part, ref.at[c, 0, 0, slot], zg_send.at[at, other], zg_recv.at[at, other], at_z(d, other))
    start(meta.at[c], meta.at[c], swap_send.at[1], swap_recv.at[1], mate)

    def z_near(slot):
        ref, at = stage(slot)
        if slot > 0:
            arrived(ref.at[c, 0, 0, at], zg_send.at[slot, 0], zg_recv.at[slot, 0])
        arrived(ref.at[1 - c, 0, 0, at], zg_send.at[slot, 1], zg_recv.at[slot, 1])

    def z_chunk(slot):
        ref, at = stage(slot)
        return ref.at[:, 0, 0, at]

    def z_pass(slot, d):
        at = SLOT_OF[DELTAS[slot] - d]
        start(z_chunk(slot), z_chunk(at), zg_send.at[at, 0], zg_recv.at[at, 0], at_z(d))

    def z_far(k):
        for slot in (SLOT_OF[-k], SLOT_OF[k])[: 1 if k == 8 else 2]:
            arrived(z_chunk(slot), zg_send.at[slot, 0], zg_recv.at[slot, 0])

    def whole(slot, piece):
        return stage_a.at[:, 0, pl.ds(1, 3), slot] if piece == 2 else stage_a.at[piece, pl.ds(1, 3), :, slot]

    def whole_start():
        for piece in range(3):
            for d in (1, -1):
                at = SLOT_OF[-d]
                start(whole(0, piece), whole(at, piece), zw_send.at[at - 1, piece], zw_recv.at[at - 1, piece], at_z(d))

    def whole_arrived():
        for piece in range(3):
            for at in (1, 2):
                arrived(whole(at, piece), zw_send.at[at - 1, piece], zw_recv.at[at - 1, piece])

    def first_at(h, g, at):
        ref, a = stage(GROUPS[g][0])
        slots = pl.ds(a, GROUPS[g][1] - GROUPS[g][0])
        return ref.at[0, 0, at, slots] if h == 0 else ref.at[1, at, 0, slots]

    def first_start(g):
        for d in (2, 1, 3):
            for h in range(2):
                sems = p1_send.at[h, g, d - 1], p1_recv.at[h, g, d - 1]
                start(first_at(h, g, 0), first_at(h, g, 4 - d), *sems, (at_x, at_y)[h](d))

    def first_arrived(g):
        for d in (1, 3, 2):
            for h in range(2):
                arrived(first_at(h, g, 4 - d), p1_send.at[h, g, d - 1], p1_recv.at[h, g, d - 1])

    def second_at(h, g, at, part):
        ref, a = stage(GROUPS[g][0])
        slots = pl.ds(a, GROUPS[g][1] - GROUPS[g][0])
        if h == 0:
            return ref.at[0, at, pl.ds(2 * part, 2), slots]
        return ref.at[1, pl.ds(2 * part, 2), at, slots]

    MOVES = ((0, 0, 1), (0, 1, 3), (0, 1, 1), (0, 0, 3), (3, 0, 1), (1, 1, 3))

    def second_start(g, k):
        at, part, d = MOVES[k]
        for h in range(2):
            sems = p2_send.at[h, g, k], p2_recv.at[h, g, k]
            start(second_at(h, g, at, part), second_at(h, g, (at + 4 - d) % 4, part), *sems, (at_y, at_x)[h](d))

    def second_arrived(g, k):
        at, part, d = MOVES[k]
        for h in range(2):
            arrived(second_at(h, g, (at + 4 - d) % 4, part), p2_send.at[h, g, k], p2_recv.at[h, g, k])

    def second_open(g):
        first_arrived(g)
        for k in range(4):
            second_start(g, k)

    def second_pass(g):
        for k in (0, 1):
            second_arrived(g, k)
            second_start(g, 4 + k)

    def halve(s, _):
        b = tiles[s]
        high = b.astype(BF)
        halves[s, :, :W] = high
        halves[s, :, W:] = (b - high.astype(F32)).astype(BF)
        return 0

    def halve_some(i):
        lax.fori_loop(i * 16, i * 16 + 16, halve, 0, unroll=2)

    flats = [ref.reshape(2 * 4 * 4 * 8 * 16, W) for ref in (stage_a, stage_b)]
    acc_rows = acc.reshape(2 * 16 * 64, W)
    rx_rows = rx.reshape(2 * 2 * 3 * 8 * 16, W)

    def products(g, h):
        def slot(k, running):
            n = plan[1, k]
            dy = (n // 16 + 4 - y) % 4
            a = flats[g][pl.ds((n // 8 % 2 * 4 + dy) * 512 + n % 8, 64, stride=8), :]
            keep = plan[2, k].astype(F32)
            high = a.astype(BF)
            a = jnp.concatenate([high, (a - high.astype(F32)).astype(BF)], axis=1)
            b = halves[plan[0, k]]
            product = jnp.dot(a, jnp.concatenate([b, b], axis=0), preferred_element_type=F32)
            running = running * keep + (product[:, :W] + product[:, W:])
            sums[k] = running
            return running

        lax.fori_loop(h * LIST, h * LIST + LIST, slot, jnp.zeros((64, W), F32), unroll=8)

        def pick(t, _):
            acc[g, t] = sums[plan[3, t]]
            return 0

        lax.fori_loop(h * 8, h * 8 + 8, pick, 0)
        for d in (2, 1, 3):
            part = acc.at[g, pl.ds(h * 8, 8), pl.ds(d * 16, 16), :]
            start(part, rx.at[g, h, 3 - d], rx_send.at[g, h, 3 - d], rx_recv.at[g, h, 3 - d], at_x(d))

    def add_up(g, h):
        for i in range(3):
            arrived(rx.at[g, h, i], rx_send.at[g, h, i], rx_recv.at[g, h, i])

        def add(s, _):
            for r in range(2):
                at = s * 2 + r
                value = acc_rows[pl.ds((g * 16 + h * 8) * 64 + at, 8, stride=64), :]
                for i in range(3):
                    value += rx_rows[pl.ds(((g * 2 + h) * 3 + i) * 128 + at, 8, stride=16), :]
                zbuf[h, g * 8 + s, r * 8 : r * 8 + 8, :] = value
            return 0

        lax.fori_loop(0, 8, add, 0, unroll=2)
        for s in sorted(range(max(g * 8, 1), g * 8 + 8), key=lambda s: -abs(DELTAS[s])):
            back = SLOT_OF[-DELTAS[s]]
            owner = {"pair": at_z(DELTAS[s])["pair"], "virt": y * 2 + h}
            start(zbuf.at[h, s], zrx.at[c, back], zr_send.at[h, back], zr_recv.at[c, back], owner)

    z_near(0)
    first_start(0)
    start(tiles_ref, tiles.at[pl.ds(c * LIST, LIST)], swap_send.at[2], swap_recv.at[2], mate)
    for k in (1, -1):
        z_near(SLOT_OF[k])
        z_pass(SLOT_OF[k], -2 * k)
    for k in (2, -2):
        z_near(SLOT_OF[k])
        z_pass(SLOT_OF[k], -k)
    first_start(1)
    for k in (1, -1, 2, -2):
        z_pass(SLOT_OF[k], -4 if k > 0 else 4)
    second_open(0)

    arrived(meta.at[1 - c], swap_send.at[1], swap_recv.at[1])
    low = lane < LIST
    both = [jnp.where(low, meta[0, k : k + 1, :], pltpu.roll(meta[1, k : k + 1, :], LIST, 1)) for k in range(2)]
    schedule(jnp.where(lane < SLOTS, both[0], 18), both[1], sched)
    turn = pltpu.make_async_copy(sched, plan, plan_sem)
    turn.start()

    z_far(3)
    z_pass(SLOT_OF[3], -4)
    z_pass(SLOT_OF[-3], 4)
    z_far(4)
    z_pass(SLOT_OF[-4], 4)
    first_start(3)
    second_pass(0)
    second_open(1)
    for k in range(2, 6):
        second_arrived(0, k)
    whole_start()
    z_far(5)
    z_far(6)
    first_start(4)
    local.wait()
    arrived(tiles.at[pl.ds((1 - c) * LIST, LIST)], swap_send.at[2], swap_recv.at[2])
    halve_some(0)
    second_pass(1)
    second_open(3)
    halve_some(1)
    z_far(7)
    z_far(8)
    first_start(2)
    halve_some(2)
    second_open(4)
    halve_some(3)
    second_pass(3)
    second_open(2)
    turn.wait()
    second_pass(4)
    for g in (3, 4):
        for k in range(2, 6):
            second_arrived(g, k)
    second_pass(2)
    products(1, 0)
    products(1, 1)
    whole_arrived()
    for g in (1, 2):
        for k in range(2, 6):
            second_arrived(g, k)
    products(0, 0)
    add_up(1, 0)
    products(0, 1)
    add_up(1, 1)
    for h in range(2):
        add_up(0, h)

    zrx[c, 0] = zbuf[c, 0]
    start(zbuf.at[1 - c, 0], zrx.at[c, 0], swap_send.at[3], swap_recv.at[3], mate)
    arrived(zrx.at[1 - c, 0], swap_send.at[3], swap_recv.at[3])
    for half in range(2):
        value = zrx[half, 0]
        for s in range(1, NZ):
            arrived(zrx.at[half, s], zr_send.at[half, s], zr_recv.at[half, s])
            value += zrx[half, s]
        fin[half] = value

    for row in range(4):
        for j in range(8):
            at = (row % 2) * 8 + j
            out_ref[row : row + 1, j * W : (j + 1) * W] = fin[row // 2, at : at + 1, :]

    for one in sent:
        one.wait_send()


def shards(t2_amplitudes, integral_tiles, out_tiles, in_tiles, tile_counts):
    vmem = pl.BlockSpec(memory_space=pltpu.VMEM)
    dma = pltpu.SemaphoreType.DMA
    return pl.pallas_call(
        kernel,
        out_shape=jax.ShapeDtypeStruct(t2_amplitudes.shape, F32),
        in_specs=[pl.BlockSpec(memory_space=pltpu.HBM)] * 4 + [vmem],
        out_specs=vmem,
        scratch_shapes=[
            pltpu.VMEM(t2_amplitudes.shape, F32),
            pltpu.VMEM(out_tiles.shape, I32),
            pltpu.VMEM(in_tiles.shape, I32),
            pltpu.VMEM((2, 16, W), F32),
            pltpu.VMEM((2, NY, NX, 8, 16, W), F32),
            pltpu.VMEM((2, NY, NX, 8, 16, W), F32),
            pltpu.VMEM((SLOTS, W, W), F32),
            pltpu.VMEM((SLOTS, W, 2 * W), BF),
            pltpu.VMEM((2, 8, W), I32),
            pltpu.VMEM((8, W), I32),
            pltpu.SMEM((8, W), I32),
            pltpu.VMEM((SLOTS + 1, 64, W), F32),
            pltpu.VMEM((2, 16, 64, W), F32),
            pltpu.VMEM((2, 2, 3, 8, 16, W), F32),
            pltpu.VMEM((2, NZ, 16, W), F32),
            pltpu.VMEM((2, NZ, 16, W), F32),
            pltpu.VMEM((2, 16, W), F32),
            dma((4,)), dma((4,)), dma, dma, dma((3,)),
            dma((NZ, 2)), dma((NZ, 2)), dma((2, 3)), dma((2, 3)), dma((2, NG, 3)), dma((2, NG, 3)), dma((2, NG, 6)), dma((2, NG, 6)),
            dma((2, 2, 3)), dma((2, 2, 3)), dma((2, NZ)), dma((2, NZ)),
        ],
        compiler_params=pltpu.CompilerParams(
            collective_id=0, has_side_effects=True, vmem_limit_bytes=62 * 1024 * 1024
        ),
    )(t2_amplitudes, integral_tiles.reshape(LIST, W, W), out_tiles, in_tiles, tile_counts)


def solution(mesh):
    return jax.shard_map(
        shards,
        mesh=mesh,
        in_specs=(
            P("pair", "virt"),
            P("pair", "virt", None, None, None),
            P("pair", "virt", None),
            P("pair", "virt", None),
            P("pair", "virt"),
        ),
        out_specs=P("pair", "virt"),
        check_vma=False,
    )
```
